32 devices in a mesh: heads: 4 (over y, x), seq: 8 (over z, core).
Axes of the slice: x: 2, y: 2, z: 4, core: 2. Of those that a mesh axis runs over, the one named last changes fastest.
Arguments:
- queries: bfloat16 [6144, 2048], P('seq', 'heads'), may hold values from -6 to 6
- key_vectors: bfloat16 [6144, 2048], P('seq', 'heads'), may hold values from -10 to 10
- value_vectors: bfloat16 [6144, 2048], P('seq', 'heads'), may hold values from -6 to 6
- random_blocks: int32 [16, 96, 3], P('heads', 'seq'), may hold values from 0 to 95, as said below
- global_blocks: int32 [2], replicated, may hold values from 0 to 95, as said below
- out_weight: bfloat16 [2048, 4096], P('heads'), may hold values from -0.1875 to 0.1875
Outputs:
- layer_out: bfloat16 [6144, 4096], P('seq', 'heads')
The draws below stay inside these ranges and needn't reach their ends.
Inputs may be any that keep to these rules, and one draw needn't show every extreme that they name: `random_blocks`: entries are block numbers. Of the entries with heads of one group of 4 and query blocks of one run of 12 blocks, at most 28 lie in any one run of key blocks s * 12 to (s + 1) * 12 - 1, and exactly 28 lie in one such run. Entries may repeat. `global_blocks`: Distinct; the last entry is the last block, 95.
All inputs are finite; a program needn't handle non-finite values.
Results may differ from the reference program's by a relative error of at most 0.0095.
Values may be sent and summed in bfloat16 or wider, within the bound.
A program may use at most 128 MiB of HBM per device.

```python
import jax
import jax.numpy as jnp
from jax import lax

D = 4096
HEADS = 16
DH = 128
BLOCK = 64
RANDOM = 3
GLOBAL = 2
HEAD_GROUPS = 4
SHARDS = 8
HEADS_DEV = 4
BLOCKS_DEV = 12
BLOCKS_ALL = 96
TOKENS = 6144
REQUESTS = 144
CAPACITY = 28
N_HEADS = 4


def global_pick(key):
    ordering = jax.random.permutation(jax.random.fold_in(key, 7), BLOCKS_ALL - 1)
    chosen = ordering[:GLOBAL - 1].astype(jnp.int32)
    last_block = jnp.full((1,), BLOCKS_ALL - 1, jnp.int32)
    return jnp.concatenate([chosen, last_block]).astype(jnp.int32)


def draw_global_blocks(key, part):
    return global_pick(key)


def draw_queries(key, part):
    drawn = jnp.clip(jax.random.normal(jax.random.fold_in(key, 21), (TOKENS, HEADS * DH), jnp.float32), -6.0, 6.0)
    return drawn.astype(jnp.bfloat16)


def draw_key_vectors(key, part):
    drawn = jax.random.normal(jax.random.fold_in(key, 22), (TOKENS, HEADS * DH), jnp.float32)
    drawn = jnp.clip(2.0 * drawn, -10.0, 10.0)
    return drawn.astype(jnp.bfloat16)


def device_lists(key):
    tickets = jnp.arange(SHARDS * CAPACITY, dtype=jnp.int32) // CAPACITY
    busiest = jax.random.randint(jax.random.fold_in(key, 1), (), 0, SHARDS).astype(jnp.int32)
    shuffled = jax.random.permutation(jax.random.fold_in(key, 2), SHARDS * CAPACITY).astype(jnp.int32)
    ranking = shuffled - jnp.where(tickets == busiest, SHARDS * CAPACITY, 0).astype(jnp.int32)
    ordering = jnp.argsort(ranking)
    owners = tickets[ordering[:REQUESTS]]
    owners = owners[jax.random.permutation(jax.random.fold_in(key, 3), REQUESTS)]
    local_ids = jax.random.randint(jax.random.fold_in(key, 4), (REQUESTS,), 0, BLOCKS_DEV).astype(jnp.int32)
    return (owners * BLOCKS_DEV + local_ids).reshape(HEADS_DEV, BLOCKS_DEV, RANDOM)


def draw_random_blocks(key, part):
    devices = HEAD_GROUPS * SHARDS
    device_keys = jax.vmap(lambda number: jax.random.fold_in(key, number))(jnp.arange(devices))
    tables = jax.vmap(device_lists)(device_keys)
    tables = tables.reshape(HEAD_GROUPS, SHARDS, HEADS_DEV, BLOCKS_DEV, RANDOM).transpose(0, 2, 1, 3, 4)
    return tables.reshape(HEADS, BLOCKS_ALL, RANDOM).astype(jnp.int32)


def with_spikes(values, stream_key, source, target, blocks, factor):
    owner, partner = [(jnp.arange(values.shape[dim]) // (values.shape[dim] // blocks)).reshape([-1 if axis == dim else 1 for axis in range(values.ndim)]) for dim in (source, target)]
    chosen = jax.random.permutation(stream_key, blocks)[partner]
    strong = (owner == chosen) | (owner == (partner + blocks // 2) % blocks)
    return jnp.where(strong, factor * values, values)


def level_of(own_key, dims, split, smallest, high):
    level = 1.0
    for axis_at, parts in split:
        steps = jax.random.uniform(jax.random.fold_in(jax.random.fold_in(own_key, 6), axis_at), (parts,), jnp.float32, smallest / len(split), high / len(split))
        level = level * jnp.repeat(jnp.exp(steps), dims[axis_at] // parts).reshape((-1,) + (1,) * (len(dims) - 1 - axis_at))
    return level


def scatter_about(stream_key, dims, deviation, bound, shards=(), kind=jnp.bfloat16):
    loudness = level_of(stream_key, dims, shards, -0.22, 0.18) if shards else 1.0
    values = jax.random.normal(stream_key, dims, jnp.float32) * deviation * loudness
    return jnp.minimum(jnp.maximum(values, -bound), bound).astype(kind)


def noise_with(own_key, extent, deviation, limit, cuts, heavy, kind=jnp.bfloat16):
    values = deviation * jax.random.normal(own_key, extent, jnp.float32)
    if cuts:
        values = values * level_of(own_key, extent, cuts, -0.22, 0.18)
    return jnp.clip(with_spikes(values, jax.random.fold_in(own_key, 3), *heavy), -limit, limit).astype(kind)


def setup_inputs(seed: int = 0) -> dict:
    splits = jax.random.split(jax.random.key(seed), 7)
    return {
        "queries": draw_queries(jax.random.fold_in(splits[6], 71), 0),
        "key_vectors": draw_key_vectors(jax.random.fold_in(splits[6], 71), 0),
        "value_vectors": scatter_about(splits[2], (TOKENS, HEADS * DH), 1.0, 6.0, ((0, 8), (1, 4))),
        "random_blocks": draw_random_blocks(jax.random.fold_in(splits[6], 71), 0),
        "global_blocks": draw_global_blocks(jax.random.fold_in(splits[6], 71), 0),
        "out_weight": noise_with(splits[5], (HEADS * DH, D), (HEADS * DH) ** -0.5, 0.1875, ((0, 4),), (0, 1, 4, 2.0)),
    }


def head_attention(operands, global_blocks):
    q_head, k_head, v_head, rand_head = operands
    block_count = q_head.shape[0] // BLOCK
    score_multiplier = DH ** -0.5
    query_block_tiles = q_head.reshape(block_count, BLOCK, DH)
    k_tiles = k_head.reshape(block_count, BLOCK, DH)
    v_tiles = v_head.reshape(block_count, BLOCK, DH)

    def gather_keys(tiles):
        zero_tile = jnp.zeros((1, BLOCK, DH), tiles.dtype)
        padded = jnp.concatenate([zero_tile, tiles, zero_tile], axis=0)
        window = jnp.stack([padded[:-2], padded[1:-1], padded[2:]], axis=1)
        random_part = tiles[rand_head]
        global_part = jnp.broadcast_to(tiles[global_blocks][None], (block_count, GLOBAL, BLOCK, DH))
        joined = jnp.concatenate([window, random_part, global_part], axis=1)
        return joined.reshape(block_count, -1, DH)

    window_key_rows = gather_keys(k_tiles)
    window_value_rows = gather_keys(v_tiles)
    logit_scores = jnp.einsum("hmo,hzo->hmz", query_block_tiles.astype(jnp.float32), window_key_rows.astype(jnp.float32)) * score_multiplier
    column_block = jnp.arange(window_key_rows.shape[1]) // BLOCK
    row_block = jnp.arange(block_count)
    valid_keys = jnp.where(column_block[None, :] == 0, row_block[:, None] > 0,
                           jnp.where(column_block[None, :] == 2, row_block[:, None] < block_count - 1, True))
    logit_scores = jnp.where(valid_keys[:, None, :], logit_scores, -jnp.inf)
    row_peak = jnp.max(logit_scores, axis=-1, keepdims=True)
    exponent = jnp.exp(logit_scores - row_peak)
    softmax_divisor = jnp.sum(exponent, axis=-1, keepdims=True)
    rounded_scores = lax.optimization_barrier(exponent.astype(jnp.bfloat16))
    sparse_result = jnp.einsum("afg,agv->afv", rounded_scores.astype(jnp.float32), window_value_rows.astype(jnp.float32)) / softmax_divisor
    sparse_result = sparse_result.astype(jnp.bfloat16)
    global_query = query_block_tiles[global_blocks].reshape(GLOBAL * BLOCK, DH)
    global_scores = jnp.dot(global_query, k_head.T, preferred_element_type=jnp.float32) * score_multiplier
    global_top = jnp.max(global_scores, axis=-1, keepdims=True)
    global_exp = jnp.exp(global_scores - global_top)
    global_out = jnp.dot(global_exp, v_head.astype(jnp.float32), precision=lax.Precision.HIGHEST)
    global_out = global_out / jnp.sum(global_exp, axis=-1, keepdims=True)
    global_out = global_out.astype(jnp.bfloat16).reshape(GLOBAL, BLOCK, DH)
    return sparse_result.at[global_blocks].set(global_out)


def reference(queries, key_vectors, value_vectors, random_blocks, global_blocks, out_weight):
    tokens_all = queries.shape[0]

    def split_heads(matrix):
        return matrix.reshape(tokens_all, HEADS, DH).transpose(1, 0, 2)

    attended = lax.map(lambda operands: head_attention(operands, global_blocks),
                       (split_heads(queries), split_heads(key_vectors), split_heads(value_vectors), random_blocks))
    merged = attended.reshape(HEADS, tokens_all, DH).transpose(1, 0, 2).reshape(tokens_all, HEADS * DH)
    group_width = HEADS_DEV * DH
    result = jnp.zeros((tokens_all, D), jnp.float32)
    for group_index in range(N_HEADS):
        start = group_index * group_width
        partial_sum = jnp.dot(merged[:, start:start + group_width], out_weight[start:start + group_width],
                              preferred_element_type=jnp.float32)
        rounded_scores = lax.optimization_barrier(partial_sum.astype(jnp.bfloat16))
        result = result + rounded_scores.astype(jnp.float32)
    return result.astype(jnp.bfloat16)
```

```python
import functools

import jax
import jax.numpy as jnp
from jax import lax
from jax.experimental import pallas as pl
from jax.experimental.pallas import tpu as pltpu
from jax.sharding import PartitionSpec as P

DH = 128
BLOCK = 64
RANDOM = 3
GLOBAL = 2


def extended(shard, sides, width):
    for axis, dim in sides:
        peers, length = (lax.axis_size(axis), shard.shape[dim])
        up = [(i, (i + 1) % peers) for i in range(peers - 1)]
        down = [(j, i) for i, j in up]
        last = lax.slice_in_dim(shard, length - width, length, axis=dim)
        leading = lax.slice_in_dim(shard, 0, width, axis=dim)
        before = lax.ppermute(last, axis, up)
        after = lax.ppermute(leading, axis, down)
        shard = jnp.concatenate([before, shard, after], axis=dim)
    return shard


def joined(shard, axis, combine):
    everything = jax.tree.map(
        lambda part, kind: lax.all_gather(part.astype(kind), axis),
        shard,
        (jnp.bfloat16, jnp.bfloat16, jnp.bfloat16),
    )

    def take(k):
        return jax.tree.map(lambda part, own: part[k].astype(own.dtype), everything, shard)

    return lax.fori_loop(
        1, lax.axis_size(axis), lambda k, so_far: combine(so_far, take(k)), take(0)
    )


def combine_parts(first, second):
    top_first, total_first, out_first = first
    top_second, total_second, out_second = second
    highest = jnp.maximum(top_first, top_second)
    scale_first = jnp.exp(top_first - highest)
    scale_second = jnp.exp(top_second - highest)
    return (
        highest,
        total_first * scale_first + total_second * scale_second,
        out_first * scale_first[..., None] + out_second * scale_second[..., None],
    )


def requested(queries, key_vectors, value_vectors, random_blocks, global_blocks, out_weight):
    shards = lax.axis_size("seq")
    my_index = lax.axis_index("seq")
    tok_rows, features = queries.shape
    heads_here = features // DH
    blocks_here = tok_rows // BLOCK
    requests = heads_here * blocks_here * RANDOM
    capacity = max(2, 3 * requests // (2 * shards) + 1)
    score_multiplier = DH ** (-0.5)
    query_block_tiles = queries.reshape(blocks_here, BLOCK, heads_here, DH).transpose(2, 0, 1, 3)
    stacked = jnp.concatenate([key_vectors, value_vectors], axis=1)
    padded = extended(stacked, (("seq", 0),), BLOCK)
    kv_tiles = padded.reshape(blocks_here + 2, BLOCK, 2, heads_here, DH).transpose(3, 0, 1, 2, 4)
    own_tiles = kv_tiles[:, 1:-1]
    table = own_tiles.reshape(heads_here * blocks_here, BLOCK, 2, DH)
    flat_lists = random_blocks.reshape(requests)
    head_of = jnp.arange(requests, dtype=jnp.int32) // (blocks_here * RANDOM)
    code_flat = head_of * blocks_here + flat_lists % blocks_here
    holders = flat_lists // blocks_here
    onehot = (holders[:, None] == jnp.arange(shards, dtype=jnp.int32)[None, :]).astype(jnp.int32)
    rank_flat = jnp.sum((jnp.cumsum(onehot, axis=0) - onehot) * onehot, axis=1)
    slot_flat = holders * capacity + rank_flat
    asked = (
        jnp.zeros((shards * capacity,), jnp.int32)
        .at[slot_flat]
        .set(code_flat)
        .reshape(shards, capacity)
    )
    arrived = lax.all_to_all(
        table[lax.all_to_all(asked, "seq", split_axis=0, concat_axis=0, tiled=True)],
        "seq",
        split_axis=0,
        concat_axis=0,
        tiled=True,
    )
    fetched = arrived.reshape(shards * capacity, BLOCK, 2, DH)[slot_flat]
    fetched = fetched.reshape(heads_here, blocks_here, RANDOM, BLOCK, 2, DH)
    holder_glob = global_blocks // blocks_here
    place_glob = global_blocks % blocks_here
    mine_glob = holder_glob == my_index
    global_q_local = query_block_tiles[:, place_glob]
    global_kv_local = own_tiles[:, place_glob]
    owned_mask = mine_glob.astype(jnp.float32)
    summed_query, summed_pairs = lax.psum(
        (
            global_q_local.astype(jnp.float32) * owned_mask[None, :, None, None],
            global_kv_local.astype(jnp.float32) * owned_mask[None, :, None, None, None],
        ),
        "seq",
    )
    global_query = summed_query.astype(jnp.bfloat16)
    global_pairs = summed_pairs.astype(jnp.bfloat16)
    window = jnp.stack([kv_tiles[:, :-2], kv_tiles[:, 1:-1], kv_tiles[:, 2:]], axis=2)
    spread_global = jnp.broadcast_to(
        global_pairs[:, None], (heads_here, blocks_here, GLOBAL, BLOCK, 2, DH)
    )
    listed = jnp.concatenate([window, fetched, spread_global], axis=2).reshape(
        heads_here, blocks_here, -1, 2, DH
    )
    window_key_rows = listed[:, :, :, 0]
    window_value_rows = listed[:, :, :, 1]
    logit_scores = (
        jnp.einsum(
            "hbqd,hbkd->hbqk",
            query_block_tiles,
            window_key_rows,
            preferred_element_type=jnp.float32,
        )
        * score_multiplier
    )
    column_block = jnp.arange(window_key_rows.shape[2]) // BLOCK
    row_global = my_index * blocks_here + jnp.arange(blocks_here)
    valid_keys = jnp.where(
        column_block[None, :] == 0,
        row_global[:, None] > 0,
        jnp.where(column_block[None, :] == 2, row_global[:, None] < shards * blocks_here - 1, True),
    )
    logit_scores = jnp.where(valid_keys[None, :, None, :], logit_scores, -jnp.inf)
    row_peak = jnp.max(logit_scores, axis=-1, keepdims=True)
    exponent = jnp.exp(logit_scores - row_peak)
    softmax_divisor = jnp.sum(exponent, axis=-1, keepdims=True)
    sparse_result = (
        jnp.einsum(
            "hbqk,hbkd->hbqd",
            exponent.astype(jnp.bfloat16),
            window_value_rows,
            preferred_element_type=jnp.float32,
        )
        / softmax_divisor
    )
    sparse_result = sparse_result.astype(jnp.bfloat16)
    local_keys = own_tiles[:, :, :, 0].reshape(heads_here, tok_rows, DH)
    local_values = own_tiles[:, :, :, 1].reshape(heads_here, tok_rows, DH).astype(jnp.float32)
    global_rows_q = global_query.reshape(heads_here, GLOBAL * BLOCK, DH)
    global_scores = (
        jnp.einsum("hqd,hkd->hqk", global_rows_q, local_keys, preferred_element_type=jnp.float32)
        * score_multiplier
    )
    local_top = jnp.max(global_scores, axis=-1)
    global_exp = jnp.exp(global_scores - local_top[..., None])
    top_all, total_all, out_all = joined(
        (
            local_top,
            jnp.sum(global_exp, axis=-1),
            jnp.einsum("hqk,hkd->hqd", global_exp, local_values, precision=lax.Precision.HIGHEST),
        ),
        "seq",
        combine_parts,
    )
    global_out = (
        (out_all / total_all[..., None]).astype(jnp.bfloat16).reshape(heads_here, GLOBAL, BLOCK, DH)
    )
    block_ids = jnp.arange(blocks_here)
    for glob_index in range(GLOBAL):
        replace_mask = mine_glob[glob_index] & (block_ids == place_glob[glob_index])
        sparse_result = jnp.where(
            replace_mask[None, :, None, None], global_out[:, glob_index][:, None], sparse_result
        )
    attention = sparse_result.transpose(1, 2, 0, 3).reshape(tok_rows, features)
    partial_out = jnp.dot(attention, out_weight, preferred_element_type=jnp.float32)
    return lax.psum_scatter(
        partial_out.astype(jnp.bfloat16), "heads", scatter_dimension=1, tiled=True
    )


MESH = pl.DeviceIdType.MESH
ANY = pl.BlockSpec(memory_space=pl.ANY)
VMEM_BYTES = 56 * 1024 * 1024


def greet(shards, groups, me, group):
    barrier = pltpu.get_barrier_semaphore()
    for k in range(1, shards):
        pl.semaphore_signal(
            barrier, inc=1, device_id={"seq": lax.rem(me + k, shards)}, device_id_type=MESH
        )
    for k in range(1, groups):
        pl.semaphore_signal(
            barrier, inc=1, device_id={"heads": lax.rem(group + k, groups)}, device_id_type=MESH
        )
    pl.semaphore_wait(barrier, shards + groups - 2)


def remote(src, dst, send, recv, device):
    return pltpu.make_async_remote_copy(
        src_ref=src,
        dst_ref=dst,
        send_sem=send,
        recv_sem=recv,
        device_id=device,
        device_id_type=MESH,
    )


def far_first(shards):
    return sorted(range(1, shards), key=lambda k: -min(k, shards - k))


def exchange_kernel(
    shards, heads, groups, rows,
    q_ref, k_ref, v_ref, list_ref, w_ref,
    q_all, k_all, v_all, list_all, w_all,
    send_sem, recv_sem, pass_send, pass_recv, w_send, w_recv, own_sem,
):
    me = lax.axis_index("seq")
    group = lax.axis_index("heads")
    share = shards // heads
    piece = rows // share
    width = w_ref.shape[1] // groups
    depth = w_ref.shape[0]
    my_head = lax.div(me, share)
    my_part = lax.rem(me, share)
    pairs = ((q_ref, q_all), (k_ref, k_all), (v_ref, v_all))

    def window(src, head, part):
        return src.at[
            pl.ds(pl.multiple_of(part * piece, piece), piece),
            pl.ds(pl.multiple_of(head * DH, DH), DH),
        ]

    def landing(dst, source, part):
        return dst.at[pl.ds(pl.multiple_of(source * rows + part * piece, piece), piece), :]

    own = [
        pltpu.make_async_copy(
            window(src, my_head, my_part), landing(dst, me, my_part), own_sem.at[t]
        )
        for t, (src, dst) in enumerate(pairs)
    ]
    own.append(pltpu.make_async_copy(list_ref.at[my_head], list_all.at[me], own_sem.at[len(pairs)]))
    for copy in own:
        copy.start()
    greet(shards, groups, me, group)

    sends = {}
    for k in far_first(shards):
        to = lax.rem(me + k, shards)
        head, part = lax.div(to, share), lax.rem(to, share)
        for t, (src, dst) in enumerate(pairs):
            sends[k, t] = remote(
                window(src, head, part),
                landing(dst, me, part),
                send_sem.at[k, t],
                recv_sem.at[k, t],
                {"seq": to},
            )
        sends[k, len(pairs)] = remote(
            list_ref.at[head],
            list_all.at[me],
            send_sem.at[k, len(pairs)],
            recv_sem.at[k, len(pairs)],
            {"seq": to},
        )
        for t in range(len(pairs) + 1):
            sends[k, t].start()
    weights = []
    for k in range(1, groups):
        to = lax.rem(group + k, groups)
        weights.append(
            remote(
                w_ref.at[:, pl.ds(pl.multiple_of(to * width, width), width)],
                w_all.at[pl.ds(pl.multiple_of(group * depth, depth), depth), :],
                w_send.at[k],
                w_recv.at[k],
                {"heads": to},
            )
        )
        weights[-1].start()

    passed = []
    for k in [0] + far_first(shards)[::-1]:
        source = lax.rem(me + shards - k, shards)
        for t, (_, dst) in enumerate(pairs):
            if k == 0:
                own[t].wait()
            else:
                sends[k, t].wait_recv()
            for j in range(1, share):
                partner = my_head * share + lax.rem(my_part + j, share)
                region = landing(dst, source, my_part)
                passed.append(
                    remote(
                        region,
                        region,
                        pass_send.at[j, k, t],
                        pass_recv.at[j, k, t],
                        {"seq": partner},
                    )
                )
                passed[-1].start()
        if k == 0:
            own[len(pairs)].wait()
        else:
            sends[k, len(pairs)].wait_recv()
    for copy in sends.values():
        copy.wait_send()
    for copy in passed:
        copy.wait()
    for copy in weights:
        copy.wait()


def attention_kernel(
    shards, heads, blocks, list_ref, glob_ref, q_ref, k_ref, v_ref, o_ref
):
    me = lax.axis_index("seq")
    share = shards // heads
    my_part = lax.rem(me, share)
    local = blocks // share
    last = shards * blocks - 1
    scale = DH ** (-0.5)
    nt = (((1,), (1,)), ((), ()))

    def block(ref, b):
        return ref[pl.ds(pl.multiple_of(b * BLOCK, BLOCK), BLOCK), :]

    lanes = (3 + RANDOM + GLOBAL) * BLOCK
    column = lax.broadcasted_iota(jnp.int32, (1, lanes), 1) // BLOCK

    def one(s, j):
        here = my_part * local + j
        b = s * blocks + here
        listed = [jnp.maximum(b - 1, 0), b, jnp.minimum(b + 1, last)]
        for r in range(RANDOM):
            at = here * RANDOM + r
            listed.append(list_ref[s, lax.div(at, 128), lax.rem(at, 128)])
        for r in range(GLOBAL):
            listed.append(glob_ref[r])
        keys = jnp.concatenate([block(k_ref, x) for x in listed], axis=0)
        values = jnp.concatenate([block(v_ref, x) for x in listed], axis=0)
        scores = lax.dot_general(
            block(q_ref, b), keys, nt, preferred_element_type=jnp.float32
        ) * scale
        hidden = ((column == 0) & (b == 0)) | ((column == 2) & (b == last))
        scores = jnp.where(hidden, -jnp.inf, scores)
        peak = jnp.max(scores, axis=-1, keepdims=True)
        weights = jnp.exp(scores - peak)
        total = jnp.sum(weights, axis=-1, keepdims=True)
        mixed = jnp.dot(
            weights.astype(jnp.bfloat16), values, preferred_element_type=jnp.float32
        )
        o_ref[pl.ds(pl.multiple_of((s * local + j) * BLOCK, BLOCK), BLOCK), :] = (
            mixed / total
        ).astype(jnp.bfloat16)

    @pl.loop(0, shards)
    def _(s):
        for j in range(local):
            one(s, j)

    glob_q = jnp.concatenate([block(q_ref, glob_ref[r]) for r in range(GLOBAL)], axis=0)
    chunk = blocks * BLOCK

    def step(c, carry):
        peak, total, mixed = carry
        at = pl.ds(pl.multiple_of(c * chunk, chunk), chunk)
        scores = lax.dot_general(
            glob_q, k_ref[at, :], nt, preferred_element_type=jnp.float32
        ) * scale
        top = jnp.maximum(peak, jnp.max(scores, axis=-1, keepdims=True))
        fade = jnp.exp(peak - top)
        weights = jnp.exp(scores - top)
        total = total * fade + jnp.sum(weights, axis=-1, keepdims=True)
        mixed = mixed * fade + jnp.dot(
            weights.astype(jnp.bfloat16), v_ref[at, :], preferred_element_type=jnp.float32
        )
        return top, total, mixed

    size = GLOBAL * BLOCK
    _, total, mixed = lax.fori_loop(
        0,
        shards,
        step,
        (
            jnp.full((size, 1), -jnp.inf, jnp.float32),
            jnp.zeros((size, 1), jnp.float32),
            jnp.zeros((size, DH), jnp.float32),
        ),
    )
    glob_out = (mixed / total).astype(jnp.bfloat16)
    for r in range(GLOBAL):
        holder = lax.div(glob_ref[r], blocks)
        place = lax.rem(glob_ref[r], blocks)

        @pl.when(lax.div(place, local) == my_part)
        def _():
            row = (holder * local + lax.rem(place, local)) * BLOCK
            o_ref[pl.ds(pl.multiple_of(row, BLOCK), BLOCK), :] = glob_out[
                r * BLOCK : (r + 1) * BLOCK, :
            ]


def project_kernel(
    shards, heads, groups,
    o_ref, w_ref, w_all, out_ref,
    att, w_here, acc, send_sem, recv_sem, pass_send, pass_recv, w_sem, own_sem,
):
    me = lax.axis_index("seq")
    group = lax.axis_index("heads")
    share = shards // heads
    rows, width = out_ref.shape
    depth = w_ref.shape[0]
    piece = rows // share
    my_head = lax.div(me, share)
    my_part = lax.rem(me, share)

    def spot(head, part):
        return att.at[
            group,
            pl.ds(pl.multiple_of(part * piece, piece), piece),
            pl.ds(pl.multiple_of(head * DH, DH), DH),
        ]

    def made(s):
        return o_ref.at[pl.ds(pl.multiple_of(s * piece, piece), piece), :]

    own = pltpu.make_async_copy(made(me), spot(my_head, my_part), own_sem)
    own.start()
    greet(shards, groups, me, group)
    sends = {}
    for k in far_first(shards):
        to = lax.rem(me + k, shards)
        sends[k] = remote(
            made(to), spot(my_head, my_part), send_sem.at[k], recv_sem.at[k], {"seq": to}
        )
        sends[k].start()
    loads = []
    for k in range(groups):
        of = lax.rem(group + groups - k, groups)
        if k == 0:
            src = w_ref.at[:, pl.ds(pl.multiple_of(group * width, width), width)]
        else:
            src = w_all.at[pl.ds(pl.multiple_of(of * depth, depth), depth), :]
        loads.append(pltpu.make_async_copy(src, w_here.at[k], w_sem.at[k]))
        loads[-1].start()

    passed = {}
    for k in [0] + far_first(shards)[::-1]:
        source = lax.rem(me + shards - k, shards)
        if k == 0:
            own.wait()
        else:
            sends[k].wait_recv()
        region = spot(lax.div(source, share), lax.rem(source, share))
        for j in range(1, groups):
            passed[j, k] = remote(
                region,
                region,
                pass_send.at[j, k],
                pass_recv.at[j, k],
                {"heads": lax.rem(group + j, groups)},
            )
            passed[j, k].start()

    tile = 256
    for j in range(groups):
        loads[j].wait()
        of = lax.rem(group + groups - j, groups)
        if j:
            for k in range(shards):
                passed[j, k].wait_recv()

        @pl.loop(0, share)
        def _(part):
            at = pl.ds(pl.multiple_of(part * piece, piece), piece)

            @pl.loop(0, width // tile)
            def _(c):
                cols = pl.ds(pl.multiple_of(c * tile, tile), tile)
                term = jnp.dot(
                    att[of, at, :], w_here[j, :, cols], preferred_element_type=jnp.float32
                )
                if j:
                    term = term + acc[at, cols]
                if j == groups - 1:
                    out_ref[at, cols] = term.astype(out_ref.dtype)
                else:
                    acc[at, cols] = term

    for copy in sends.values():
        copy.wait_send()
    for copy in passed.values():
        copy.wait_send()


def regrouped(queries, key_vectors, value_vectors, random_blocks, global_blocks, out_weight):
    shards = lax.axis_size("seq")
    groups = lax.axis_size("heads")
    rows, features = queries.shape
    heads = features // DH
    blocks = rows // BLOCK
    share = shards // heads
    piece = rows // share
    depth, model = out_weight.shape
    width = model // groups
    entries = blocks * RANDOM
    tall = -(-entries // 1024) * 8
    lists = jnp.pad(
        random_blocks.reshape(heads, entries), ((0, 0), (0, tall * 128 - entries))
    ).reshape(heads, tall, 128)
    dma = pltpu.SemaphoreType.DMA
    bf16 = jnp.bfloat16
    whole = jax.ShapeDtypeStruct((shards * rows, DH), bf16)
    q_all, k_all, v_all, list_all, w_all = pl.pallas_call(
        functools.partial(exchange_kernel, shards, heads, groups, rows),
        out_shape=(
            whole,
            whole,
            whole,
            jax.ShapeDtypeStruct((shards, tall, 128), jnp.int32),
            jax.ShapeDtypeStruct((groups * depth, width), bf16),
        ),
        in_specs=[ANY] * 5,
        out_specs=(ANY,) * 5,
        scratch_shapes=[
            dma((shards, 4)),
            dma((shards, 4)),
            dma((share, shards, 3)),
            dma((share, shards, 3)),
            dma((groups,)),
            dma((groups,)),
            dma((4,)),
        ],
        compiler_params=pltpu.CompilerParams(
            collective_id=0, has_side_effects=True, vmem_limit_bytes=VMEM_BYTES
        ),
        name="exchange",
    )(queries, key_vectors, value_vectors, lists, out_weight)
    vmem = pl.BlockSpec(memory_space=pltpu.VMEM)
    smem = pl.BlockSpec(memory_space=pltpu.SMEM)
    mixed = pl.pallas_call(
        functools.partial(attention_kernel, shards, heads, blocks),
        out_shape=jax.ShapeDtypeStruct((shards * piece, DH), bf16),
        in_specs=[smem, smem, vmem, vmem, vmem],
        out_specs=vmem,
        compiler_params=pltpu.CompilerParams(vmem_limit_bytes=VMEM_BYTES),
        name="attention",
    )(list_all, global_blocks, q_all, k_all, v_all)
    return pl.pallas_call(
        functools.partial(project_kernel, shards, heads, groups),
        out_shape=jax.ShapeDtypeStruct((rows, width), bf16),
        in_specs=[ANY] * 3,
        out_specs=vmem,
        scratch_shapes=[
            pltpu.VMEM((groups, rows, features), bf16),
            pltpu.VMEM((groups, depth, width), bf16),
            pltpu.VMEM((rows, width), jnp.float32),
            dma((shards,)),
            dma((shards,)),
            dma((groups, shards)),
            dma((groups, shards)),
            dma((groups,)),
            dma,
        ],
        compiler_params=pltpu.CompilerParams(
            collective_id=1, has_side_effects=True, vmem_limit_bytes=VMEM_BYTES
        ),
        name="project",
    )(mixed, out_weight, w_all)


def on_device(queries, key_vectors, value_vectors, random_blocks, global_blocks, out_weight):
    shards = lax.axis_size("seq")
    rows, features = queries.shape
    heads = features // DH
    whole_heads = shards % heads == 0 and (rows // BLOCK) % (shards // heads) == 0
    body = regrouped if whole_heads else requested
    return body(queries, key_vectors, value_vectors, random_blocks, global_blocks, out_weight)


def solution(mesh):
    placed = (
        P("seq", "heads"),
        P("seq", "heads"),
        P("seq", "heads"),
        P("heads", "seq", None),
        P(),
        P("heads", None),
    )
    return jax.shard_map(
        on_device, mesh=mesh, in_specs=placed, out_specs=P("seq", "heads"), check_vma=False
    )
```

```python
import functools

import jax
import jax.numpy as jnp
from jax import lax
from jax.experimental import pallas as pl
from jax.experimental.pallas import tpu as pltpu
from jax.sharding import PartitionSpec as P

DH = 128
BLOCK = 64
RANDOM = 3
GLOBAL = 2


def extended(shard, sides, width):
    for axis, dim in sides:
        peers, length = (lax.axis_size(axis), shard.shape[dim])
        up = [(i, (i + 1) % peers) for i in range(peers - 1)]
        down = [(j, i) for i, j in up]
        last = lax.slice_in_dim(shard, length - width, length, axis=dim)
        leading = lax.slice_in_dim(shard, 0, width, axis=dim)
        before = lax.ppermute(last, axis, up)
        after = lax.ppermute(leading, axis, down)
        shard = jnp.concatenate([before, shard, after], axis=dim)
    return shard


def joined(shard, axis, combine):
    everything = jax.tree.map(
        lambda part, kind: lax.all_gather(part.astype(kind), axis),
        shard,
        (jnp.bfloat16, jnp.bfloat16, jnp.bfloat16),
    )

    def take(k):
        return jax.tree.map(lambda part, own: part[k].astype(own.dtype), everything, shard)

    return lax.fori_loop(
        1, lax.axis_size(axis), lambda k, so_far: combine(so_far, take(k)), take(0)
    )


def combine_parts(first, second):
    top_first, total_first, out_first = first
    top_second, total_second, out_second = second
    highest = jnp.maximum(top_first, top_second)
    scale_first = jnp.exp(top_first - highest)
    scale_second = jnp.exp(top_second - highest)
    return (
        highest,
        total_first * scale_first + total_second * scale_second,
        out_first * scale_first[..., None] + out_second * scale_second[..., None],
    )


def requested(queries, key_vectors, value_vectors, random_blocks, global_blocks, out_weight):
    shards = lax.axis_size("seq")
    my_index = lax.axis_index("seq")
    tok_rows, features = queries.shape
    heads_here = features // DH
    blocks_here = tok_rows // BLOCK
    requests = heads_here * blocks_here * RANDOM
    capacity = max(2, 3 * requests // (2 * shards) + 1)
    score_multiplier = DH ** (-0.5)
    query_block_tiles = queries.reshape(blocks_here, BLOCK, heads_here, DH).transpose(2, 0, 1, 3)
    stacked = jnp.concatenate([key_vectors, value_vectors], axis=1)
    padded = extended(stacked, (("seq", 0),), BLOCK)
    kv_tiles = padded.reshape(blocks_here + 2, BLOCK, 2, heads_here, DH).transpose(3, 0, 1, 2, 4)
    own_tiles = kv_tiles[:, 1:-1]
    table = own_tiles.reshape(heads_here * blocks_here, BLOCK, 2, DH)
    flat_lists = random_blocks.reshape(requests)
    head_of = jnp.arange(requests, dtype=jnp.int32) // (blocks_here * RANDOM)
    code_flat = head_of * blocks_here + flat_lists % blocks_here
    holders = flat_lists // blocks_here
    onehot = (holders[:, None] == jnp.arange(shards, dtype=jnp.int32)[None, :]).astype(jnp.int32)
    rank_flat = jnp.sum((jnp.cumsum(onehot, axis=0) - onehot) * onehot, axis=1)
    slot_flat = holders * capacity + rank_flat
    asked = (
        jnp.zeros((shards * capacity,), jnp.int32)
        .at[slot_flat]
        .set(code_flat)
        .reshape(shards, capacity)
    )
    arrived = lax.all_to_all(
        table[lax.all_to_all(asked, "seq", split_axis=0, concat_axis=0, tiled=True)],
        "seq",
        split_axis=0,
        concat_axis=0,
        tiled=True,
    )
    fetched = arrived.reshape(shards * capacity, BLOCK, 2, DH)[slot_flat]
    fetched = fetched.reshape(heads_here, blocks_here, RANDOM, BLOCK, 2, DH)
    holder_glob = global_blocks // blocks_here
    place_glob = global_blocks % blocks_here
    mine_glob = holder_glob == my_index
    global_q_local = query_block_tiles[:, place_glob]
    global_kv_local = own_tiles[:, place_glob]
    owned_mask = mine_glob.astype(jnp.float32)
    summed_query, summed_pairs = lax.psum(
        (
            global_q_local.astype(jnp.float32) * owned_mask[None, :, None, None],
            global_kv_local.astype(jnp.float32) * owned_mask[None, :, None, None, None],
        ),
        "seq",
    )
    global_query = summed_query.astype(jnp.bfloat16)
    global_pairs = summed_pairs.astype(jnp.bfloat16)
    window = jnp.stack([kv_tiles[:, :-2], kv_tiles[:, 1:-1], kv_tiles[:, 2:]], axis=2)
    spread_global = jnp.broadcast_to(
        global_pairs[:, None], (heads_here, blocks_here, GLOBAL, BLOCK, 2, DH)
    )
    listed = jnp.concatenate([window, fetched, spread_global], axis=2).reshape(
        heads_here, blocks_here, -1, 2, DH
    )
    window_key_rows = listed[:, :, :, 0]
    window_value_rows = listed[:, :, :, 1]
    logit_scores = (
        jnp.einsum(
            "hbqd,hbkd->hbqk",
            query_block_tiles,
            window_key_rows,
            preferred_element_type=jnp.float32,
        )
        * score_multiplier
    )
    column_block = jnp.arange(window_key_rows.shape[2]) // BLOCK
    row_global = my_index * blocks_here + jnp.arange(blocks_here)
    valid_keys = jnp.where(
        column_block[None, :] == 0,
        row_global[:, None] > 0,
        jnp.where(column_block[None, :] == 2, row_global[:, None] < shards * blocks_here - 1, True),
    )
    logit_scores = jnp.where(valid_keys[None, :, None, :], logit_scores, -jnp.inf)
    row_peak = jnp.max(logit_scores, axis=-1, keepdims=True)
    exponent = jnp.exp(logit_scores - row_peak)
    softmax_divisor = jnp.sum(exponent, axis=-1, keepdims=True)
    sparse_result = (
        jnp.einsum(
            "hbqk,hbkd->hbqd",
            exponent.astype(jnp.bfloat16),
            window_value_rows,
            preferred_element_type=jnp.float32,
        )
        / softmax_divisor
    )
    sparse_result = sparse_result.astype(jnp.bfloat16)
    local_keys = own_tiles[:, :, :, 0].reshape(heads_here, tok_rows, DH)
    local_values = own_tiles[:, :, :, 1].reshape(heads_here, tok_rows, DH).astype(jnp.float32)
    global_rows_q = global_query.reshape(heads_here, GLOBAL * BLOCK, DH)
    global_scores = (
        jnp.einsum("hqd,hkd->hqk", global_rows_q, local_keys, preferred_element_type=jnp.float32)
        * score_multiplier
    )
    local_top = jnp.max(global_scores, axis=-1)
    global_exp = jnp.exp(global_scores - local_top[..., None])
    top_all, total_all, out_all = joined(
        (
            local_top,
            jnp.sum(global_exp, axis=-1),
            jnp.einsum("hqk,hkd->hqd", global_exp, local_values, precision=lax.Precision.HIGHEST),
        ),
        "seq",
        combine_parts,
    )
    global_out = (
        (out_all / total_all[..., None]).astype(jnp.bfloat16).reshape(heads_here, GLOBAL, BLOCK, DH)
    )
    block_ids = jnp.arange(blocks_here)
    for glob_index in range(GLOBAL):
        replace_mask = mine_glob[glob_index] & (block_ids == place_glob[glob_index])
        sparse_result = jnp.where(
            replace_mask[None, :, None, None], global_out[:, glob_index][:, None], sparse_result
        )
    attention = sparse_result.transpose(1, 2, 0, 3).reshape(tok_rows, features)
    partial_out = jnp.dot(attention, out_weight, preferred_element_type=jnp.float32)
    return lax.psum_scatter(
        partial_out.astype(jnp.bfloat16), "heads", scatter_dimension=1, tiled=True
    )


MESH = pl.DeviceIdType.MESH
ANY = pl.BlockSpec(memory_space=pl.ANY)
VMEM_BYTES = 56 * 1024 * 1024
SIDE = 2
TILE = 256
LAG = 2


def greet(shards, groups, me, group):
    barrier = pltpu.get_barrier_semaphore()
    for k in range(1, shards):
        pl.semaphore_signal(
            barrier, inc=1, device_id={"seq": lax.rem(me + k, shards)}, device_id_type=MESH
        )
    for k in range(1, groups):
        pl.semaphore_signal(
            barrier, inc=1, device_id={"heads": lax.rem(group + k, groups)}, device_id_type=MESH
        )
    pl.semaphore_wait(barrier, shards + groups - 2)


def remote(src, dst, send, recv, device):
    return pltpu.make_async_remote_copy(
        src_ref=src,
        dst_ref=dst,
        send_sem=send,
        recv_sem=recv,
        device_id=device,
        device_id_type=MESH,
    )


def far_first(shards):
    return sorted(range(1, shards), key=lambda k: -min(k, shards - k))


def layer_kernel(
    shards, heads, groups,
    q_ref, k_ref, v_ref, list_ref, glob_ref, w_ref, out_ref,
    q_all, k_all, v_all, list_all, list_here, w_here, glob_here, o_here, att, acc,
    send_sem, recv_sem, pass_send, pass_recv, w_send, w_recv, own_sem,
    o_send, o_recv, side_send, side_recv, half_send, half_recv,
):
    me = lax.axis_index("seq")
    group = lax.axis_index("heads")
    rows, width = out_ref.shape
    share = shards // heads
    piece = rows // share
    blocks = rows // BLOCK
    local = blocks // share
    last = shards * blocks - 1
    scale = DH ** (-0.5)
    nt = (((1,), (1,)), ((), ()))
    my_head = lax.div(me, share)
    my_part = lax.rem(me, share)
    pairs = ((q_ref, q_all), (k_ref, k_all), (v_ref, v_all))
    count = len(pairs)

    def window(src, head, part):
        return src.at[
            pl.ds(part * local, local), :, pl.ds(pl.multiple_of(head * DH, DH), DH)
        ]

    def landing(dst, source, part):
        return dst.at[pl.ds(source * blocks + part * local, local)]

    own = [
        pltpu.make_async_copy(
            window(src, my_head, my_part), landing(dst, me, my_part), own_sem.at[t]
        )
        for t, (src, dst) in enumerate(pairs)
    ]
    own.append(pltpu.make_async_copy(list_ref.at[my_head], list_all.at[me], own_sem.at[count]))
    own.append(
        pltpu.make_async_copy(
            w_ref.at[:, pl.ds(pl.multiple_of(group * width, width), width)],
            w_here.at[group],
            own_sem.at[count + 1],
        )
    )
    for copy in own:
        copy.start()
    greet(shards, groups, me, group)

    sends = {}
    for k in far_first(shards):
        to = lax.rem(me + k, shards)
        head, part = lax.div(to, share), lax.rem(to, share)
        for t, (src, dst) in enumerate(pairs):
            sends[k, t] = remote(
                window(src, head, part),
                landing(dst, me, part),
                send_sem.at[k, t],
                recv_sem.at[k, t],
                {"seq": to},
            )
        sends[k, count] = remote(
            list_ref.at[head],
            list_all.at[me],
            send_sem.at[k, count],
            recv_sem.at[k, count],
            {"seq": to},
        )
        for t in range(count + 1):
            sends[k, t].start()
    weights = []
    for k in range(1, groups):
        to = lax.rem(group + k, groups)
        weights.append(
            remote(
                w_ref.at[:, pl.ds(pl.multiple_of(to * width, width), width)],
                w_here.at[group],
                w_send.at[k],
                w_recv.at[k],
                {"heads": to},
            )
        )
        weights[-1].start()

    passed = []
    for k in [0] + far_first(shards)[::-1]:
        source = lax.rem(me + shards - k, shards)
        for t, (_, dst) in enumerate(pairs):
            if k == 0:
                own[t].wait()
            else:
                sends[k, t].wait_recv()
            for j in range(1, share):
                partner = my_head * share + lax.rem(my_part + j, share)
                region = landing(dst, source, my_part)
                passed.append(
                    remote(
                        region,
                        region,
                        pass_send.at[j, k, t],
                        pass_recv.at[j, k, t],
                        {"seq": partner},
                    )
                )
                passed[-1].start()
        if k == 0:
            own[count].wait()
        else:
            sends[k, count].wait_recv()
    told = pltpu.make_async_copy(list_all, list_here, own_sem.at[count])
    told.start()
    for copy in passed:
        copy.wait_recv()
    told.wait()

    glob_q = jnp.concatenate([q_all[glob_ref[r]] for r in range(GLOBAL)], axis=0)

    def step(c, carry):
        peak, total, mixed = carry
        at = pl.ds(c * blocks, blocks)
        scores = lax.dot_general(
            glob_q, k_all[at].reshape(rows, DH), nt, preferred_element_type=jnp.float32
        ) * scale
        top = jnp.maximum(peak, jnp.max(scores, axis=-1, keepdims=True))
        fade = jnp.exp(peak - top)
        heavy = jnp.exp(scores - top)
        total = total * fade + jnp.sum(heavy, axis=-1, keepdims=True)
        mixed = mixed * fade + jnp.dot(
            heavy.astype(jnp.bfloat16),
            v_all[at].reshape(rows, DH),
            preferred_element_type=jnp.float32,
        )
        return top, total, mixed

    size = GLOBAL * BLOCK
    _, total_glob, mixed_glob = lax.fori_loop(
        0,
        shards,
        step,
        (
            jnp.full((size, 1), -jnp.inf, jnp.float32),
            jnp.zeros((size, 1), jnp.float32),
            jnp.zeros((size, DH), jnp.float32),
        ),
    )
    glob_here[...] = mixed_glob / total_glob

    lanes = (3 + RANDOM + GLOBAL) * BLOCK
    column = lax.broadcasted_iota(jnp.int32, (1, lanes), 1) // BLOCK

    def one(i, s, j):
        here = my_part * local + j
        b = s * blocks + here
        listed = [jnp.maximum(b - 1, 0), b, jnp.minimum(b + 1, last)]
        for r in range(RANDOM):
            at = here * RANDOM + r
            listed.append(list_here[s, lax.div(at, 128), lax.rem(at, 128)])
        for r in range(GLOBAL):
            listed.append(glob_ref[r])
        keys = jnp.concatenate([k_all[x] for x in listed], axis=0)
        values = jnp.concatenate([v_all[x] for x in listed], axis=0)
        scores = lax.dot_general(
            q_all[b], keys, nt, preferred_element_type=jnp.float32
        ) * scale
        hidden = ((column == 0) & (b == 0)) | ((column == 2) & (b == last))
        scores = jnp.where(hidden, -jnp.inf, scores)
        peak = jnp.max(scores, axis=-1, keepdims=True)
        heavy = jnp.exp(scores - peak)
        total = jnp.sum(heavy, axis=-1, keepdims=True)
        mixed = jnp.dot(heavy.astype(jnp.bfloat16), values, preferred_element_type=jnp.float32)
        result = mixed / total
        for r in range(GLOBAL):
            apart = jnp.full((BLOCK, DH), b, jnp.int32) - jnp.full((BLOCK, DH), glob_ref[r], jnp.int32)
            result = jnp.where(apart == 0, glob_here[r * BLOCK : (r + 1) * BLOCK, :], result)
        o_here[i, j * BLOCK : (j + 1) * BLOCK, :] = result.astype(jnp.bfloat16)

    stride = 3 if shards % 3 else 1
    across = lax.div(group, SIDE)
    along = lax.rem(group, SIDE)
    sides = (across * SIDE + (1 - along), (1 - across) * SIDE + along)
    diagonal = (1 - across) * SIDE + (1 - along)

    def spot(of, source):
        part = lax.rem(source, share)
        return att.at[
            of,
            pl.ds(pl.multiple_of(part * piece, piece), piece),
            pl.ds(pl.multiple_of(lax.div(source, share) * DH, DH), DH),
        ]

    def ahead(i):
        return lax.rem(me + lax.rem(i * stride, shards), shards)

    def behind(i):
        return lax.rem(me + shards - lax.rem(i * stride, shards), shards)

    def kept():
        return pltpu.make_async_copy(o_here.at[0], spot(group, me), own_sem.at[0])

    def back(i):
        return remote(
            o_here.at[i], spot(group, me), o_send.at[i], o_recv.at[i], {"seq": ahead(i)}
        )

    def sideways(i, n):
        region = spot(group, behind(i))
        return remote(
            region, region, side_send.at[n, i], side_recv.at[n, i], {"heads": sides[n]}
        )

    def corner(i, n):
        half = piece // 2
        region = spot(sides[n], behind(i)).at[n * half : (n + 1) * half, :]
        return remote(
            region, region, half_send.at[n, i], half_recv.at[n, i], {"heads": sides[1 - n]}
        )

    @pl.loop(0, shards + 2 * LAG)
    def _(i):
        @pl.when(i < shards)
        def _():
            s = ahead(i)
            for j in range(local):
                one(i, s, j)

            @pl.when(i == 0)
            def _():
                kept().start()

            @pl.when(i > 0)
            def _():
                back(i).start()

        @pl.when((i >= LAG) & (i < shards + LAG))
        def _():
            due = i - LAG

            @pl.when(due == 0)
            def _():
                kept().wait()

            @pl.when(due > 0)
            def _():
                back(due).wait_recv()

            for n in range(SIDE):
                sideways(due, n).start()

        @pl.when(i >= 2 * LAG)
        def _():
            due = i - 2 * LAG
            for n in range(SIDE):
                sideways(due, n).wait_recv()
                corner(due, n).start()

    own[count + 1].wait()
    for copy in weights:
        copy.wait_recv()
    turns = (group, *sides, diagonal)
    for turn, of in enumerate(turns):
        if turn == len(turns) - 1:

            @pl.loop(0, shards)
            def _(i):
                for n in range(SIDE):
                    corner(i, n).wait_recv()

        @pl.loop(0, share)
        def _(part):
            at = pl.ds(pl.multiple_of(part * piece, piece), piece)

            @pl.loop(0, width // TILE)
            def _(c):
                cols = pl.ds(pl.multiple_of(c * TILE, TILE), TILE)
                term = jnp.dot(
                    att[of, at, :], w_here[of, :, cols], preferred_element_type=jnp.float32
                )
                if turn:
                    term = term + acc[at, cols]
                if turn == len(turns) - 1:
                    out_ref[at, cols] = term.astype(out_ref.dtype)
                else:
                    acc[at, cols] = term

    for copy in sends.values():
        copy.wait_send()
    for copy in passed:
        copy.wait_send()
    for copy in weights:
        copy.wait_send()

    @pl.loop(0, shards)
    def _(i):
        @pl.when(i > 0)
        def _():
            back(i).wait_send()

        for n in range(SIDE):
            sideways(i, n).wait_send()
            corner(i, n).wait_send()


def regrouped(queries, key_vectors, value_vectors, random_blocks, global_blocks, out_weight):
    shards = lax.axis_size("seq")
    groups = lax.axis_size("heads")
    rows, features = queries.shape
    heads = features // DH
    blocks = rows // BLOCK
    share = shards // heads
    piece = rows // share
    depth, model = out_weight.shape
    width = model // groups
    entries = blocks * RANDOM
    tall = -(-entries // 1024) * 8
    lists = jnp.pad(
        random_blocks.reshape(heads, entries), ((0, 0), (0, tall * 128 - entries))
    ).reshape(heads, tall, 128)
    dma = pltpu.SemaphoreType.DMA
    bf16 = jnp.bfloat16
    whole = pltpu.VMEM((shards * blocks, BLOCK, DH), bf16)
    split = (blocks, BLOCK, features)
    return pl.pallas_call(
        functools.partial(layer_kernel, shards, heads, groups),
        out_shape=jax.ShapeDtypeStruct((rows, width), bf16),
        in_specs=[ANY] * 4 + [pl.BlockSpec(memory_space=pltpu.SMEM), ANY],
        out_specs=pl.BlockSpec(memory_space=pltpu.VMEM),
        scratch_shapes=[
            whole,
            whole,
            whole,
            pltpu.VMEM((shards, tall, 128), jnp.int32),
            pltpu.SMEM((shards, tall, 128), jnp.int32),
            pltpu.VMEM((groups, depth, width), bf16),
            pltpu.VMEM((GLOBAL * BLOCK, DH), jnp.float32),
            pltpu.VMEM((shards, piece, DH), bf16),
            pltpu.VMEM((groups, rows, features), bf16),
            pltpu.VMEM((rows, width), jnp.float32),
            dma((shards, 4)),
            dma((shards, 4)),
            dma((share, shards, 3)),
            dma((share, shards, 3)),
            dma((groups,)),
            dma((groups,)),
            dma((5,)),
            dma((shards,)),
            dma((shards,)),
            dma((SIDE, shards)),
            dma((SIDE, shards)),
            dma((SIDE, shards)),
            dma((SIDE, shards)),
        ],
        compiler_params=pltpu.CompilerParams(
            collective_id=0, has_side_effects=True, vmem_limit_bytes=VMEM_BYTES
        ),
        name="layer",
    )(
        queries.reshape(split),
        key_vectors.reshape(split),
        value_vectors.reshape(split),
        lists,
        global_blocks,
        out_weight,
    )


def on_device(queries, key_vectors, value_vectors, random_blocks, global_blocks, out_weight):
    shards = lax.axis_size("seq")
    groups = lax.axis_size("heads")
    rows, features = queries.shape
    heads = features // DH
    whole_heads = shards % heads == 0 and (rows // BLOCK) % (shards // heads) == 0
    body = regrouped if whole_heads and groups == SIDE * SIDE else requested
    return body(queries, key_vectors, value_vectors, random_blocks, global_blocks, out_weight)


def solution(mesh):
    placed = (
        P("seq", "heads"),
        P("seq", "heads"),
        P("seq", "heads"),
        P("heads", "seq", None),
        P(),
        P("heads", None),
    )
    return jax.shard_map(
        on_device, mesh=mesh, in_specs=placed, out_specs=P("seq", "heads"), check_vma=False
    )
```

```python
import functools

import jax
import jax.numpy as jnp
from jax import lax
from jax.experimental import pallas as pl
from jax.experimental.pallas import tpu as pltpu
from jax.sharding import PartitionSpec as P

DH = 128
BLOCK = 64
RANDOM = 3
GLOBAL = 2


def extended(shard, sides, width):
    for axis, dim in sides:
        peers, length = (lax.axis_size(axis), shard.shape[dim])
        up = [(i, (i + 1) % peers) for i in range(peers - 1)]
        down = [(j, i) for i, j in up]
        last = lax.slice_in_dim(shard, length - width, length, axis=dim)
        leading = lax.slice_in_dim(shard, 0, width, axis=dim)
        before = lax.ppermute(last, axis, up)
        after = lax.ppermute(leading, axis, down)
        shard = jnp.concatenate([before, shard, after], axis=dim)
    return shard


def joined(shard, axis, combine):
    everything = jax.tree.map(
        lambda part, kind: lax.all_gather(part.astype(kind), axis),
        shard,
        (jnp.bfloat16, jnp.bfloat16, jnp.bfloat16),
    )

    def take(k):
        return jax.tree.map(lambda part, own: part[k].astype(own.dtype), everything, shard)

    return lax.fori_loop(
        1, lax.axis_size(axis), lambda k, so_far: combine(so_far, take(k)), take(0)
    )


def combine_parts(first, second):
    top_first, total_first, out_first = first
    top_second, total_second, out_second = second
    highest = jnp.maximum(top_first, top_second)
    scale_first = jnp.exp(top_first - highest)
    scale_second = jnp.exp(top_second - highest)
    return (
        highest,
        total_first * scale_first + total_second * scale_second,
        out_first * scale_first[..., None] + out_second * scale_second[..., None],
    )


def requested(queries, key_vectors, value_vectors, random_blocks, global_blocks, out_weight):
    shards = lax.axis_size("seq")
    my_index = lax.axis_index("seq")
    tok_rows, features = queries.shape
    heads_here = features // DH
    blocks_here = tok_rows // BLOCK
    requests = heads_here * blocks_here * RANDOM
    capacity = max(2, 3 * requests // (2 * shards) + 1)
    score_multiplier = DH ** (-0.5)
    query_block_tiles = queries.reshape(blocks_here, BLOCK, heads_here, DH).transpose(2, 0, 1, 3)
    stacked = jnp.concatenate([key_vectors, value_vectors], axis=1)
    padded = extended(stacked, (("seq", 0),), BLOCK)
    kv_tiles = padded.reshape(blocks_here + 2, BLOCK, 2, heads_here, DH).transpose(3, 0, 1, 2, 4)
    own_tiles = kv_tiles[:, 1:-1]
    table = own_tiles.reshape(heads_here * blocks_here, BLOCK, 2, DH)
    flat_lists = random_blocks.reshape(requests)
    head_of = jnp.arange(requests, dtype=jnp.int32) // (blocks_here * RANDOM)
    code_flat = head_of * blocks_here + flat_lists % blocks_here
    holders = flat_lists // blocks_here
    onehot = (holders[:, None] == jnp.arange(shards, dtype=jnp.int32)[None, :]).astype(jnp.int32)
    rank_flat = jnp.sum((jnp.cumsum(onehot, axis=0) - onehot) * onehot, axis=1)
    slot_flat = holders * capacity + rank_flat
    asked = (
        jnp.zeros((shards * capacity,), jnp.int32)
        .at[slot_flat]
        .set(code_flat)
        .reshape(shards, capacity)
    )
    arrived = lax.all_to_all(
        table[lax.all_to_all(asked, "seq", split_axis=0, concat_axis=0, tiled=True)],
        "seq",
        split_axis=0,
        concat_axis=0,
        tiled=True,
    )
    fetched = arrived.reshape(shards * capacity, BLOCK, 2, DH)[slot_flat]
    fetched = fetched.reshape(heads_here, blocks_here, RANDOM, BLOCK, 2, DH)
    holder_glob = global_blocks // blocks_here
    place_glob = global_blocks % blocks_here
    mine_glob = holder_glob == my_index
    global_q_local = query_block_tiles[:, place_glob]
    global_kv_local = own_tiles[:, place_glob]
    owned_mask = mine_glob.astype(jnp.float32)
    summed_query, summed_pairs = lax.psum(
        (
            global_q_local.astype(jnp.float32) * owned_mask[None, :, None, None],
            global_kv_local.astype(jnp.float32) * owned_mask[None, :, None, None, None],
        ),
        "seq",
    )
    global_query = summed_query.astype(jnp.bfloat16)
    global_pairs = summed_pairs.astype(jnp.bfloat16)
    window = jnp.stack([kv_tiles[:, :-2], kv_tiles[:, 1:-1], kv_tiles[:, 2:]], axis=2)
    spread_global = jnp.broadcast_to(
        global_pairs[:, None], (heads_here, blocks_here, GLOBAL, BLOCK, 2, DH)
    )
    listed = jnp.concatenate([window, fetched, spread_global], axis=2).reshape(
        heads_here, blocks_here, -1, 2, DH
    )
    window_key_rows = listed[:, :, :, 0]
    window_value_rows = listed[:, :, :, 1]
    logit_scores = (
        jnp.einsum(
            "hbqd,hbkd->hbqk",
            query_block_tiles,
            window_key_rows,
            preferred_element_type=jnp.float32,
        )
        * score_multiplier
    )
    column_block = jnp.arange(window_key_rows.shape[2]) // BLOCK
    row_global = my_index * blocks_here + jnp.arange(blocks_here)
    valid_keys = jnp.where(
        column_block[None, :] == 0,
        row_global[:, None] > 0,
        jnp.where(column_block[None, :] == 2, row_global[:, None] < shards * blocks_here - 1, True),
    )
    logit_scores = jnp.where(valid_keys[None, :, None, :], logit_scores, -jnp.inf)
    row_peak = jnp.max(logit_scores, axis=-1, keepdims=True)
    exponent = jnp.exp(logit_scores - row_peak)
    softmax_divisor = jnp.sum(exponent, axis=-1, keepdims=True)
    sparse_result = (
        jnp.einsum(
            "hbqk,hbkd->hbqd",
            exponent.astype(jnp.bfloat16),
            window_value_rows,
            preferred_element_type=jnp.float32,
        )
        / softmax_divisor
    )
    sparse_result = sparse_result.astype(jnp.bfloat16)
    local_keys = own_tiles[:, :, :, 0].reshape(heads_here, tok_rows, DH)
    local_values = own_tiles[:, :, :, 1].reshape(heads_here, tok_rows, DH).astype(jnp.float32)
    global_rows_q = global_query.reshape(heads_here, GLOBAL * BLOCK, DH)
    global_scores = (
        jnp.einsum("hqd,hkd->hqk", global_rows_q, local_keys, preferred_element_type=jnp.float32)
        * score_multiplier
    )
    local_top = jnp.max(global_scores, axis=-1)
    global_exp = jnp.exp(global_scores - local_top[..., None])
    top_all, total_all, out_all = joined(
        (
            local_top,
            jnp.sum(global_exp, axis=-1),
            jnp.einsum("hqk,hkd->hqd", global_exp, local_values, precision=lax.Precision.HIGHEST),
        ),
        "seq",
        combine_parts,
    )
    global_out = (
        (out_all / total_all[..., None]).astype(jnp.bfloat16).reshape(heads_here, GLOBAL, BLOCK, DH)
    )
    block_ids = jnp.arange(blocks_here)
    for glob_index in range(GLOBAL):
        replace_mask = mine_glob[glob_index] & (block_ids == place_glob[glob_index])
        sparse_result = jnp.where(
            replace_mask[None, :, None, None], global_out[:, glob_index][:, None], sparse_result
        )
    attention = sparse_result.transpose(1, 2, 0, 3).reshape(tok_rows, features)
    partial_out = jnp.dot(attention, out_weight, preferred_element_type=jnp.float32)
    return lax.psum_scatter(
        partial_out.astype(jnp.bfloat16), "heads", scatter_dimension=1, tiled=True
    )


MESH = pl.DeviceIdType.MESH
ANY = pl.BlockSpec(memory_space=pl.ANY)
VMEM_BYTES = 56 * 1024 * 1024
SIDE = 2
TILE = 256
LAG = 2


def greet(shards, groups, me, group):
    barrier = pltpu.get_barrier_semaphore()
    for k in range(1, shards):
        pl.semaphore_signal(
            barrier, inc=1, device_id={"seq": lax.rem(me + k, shards)}, device_id_type=MESH
        )
    for k in range(1, groups):
        pl.semaphore_signal(
            barrier, inc=1, device_id={"heads": lax.rem(group + k, groups)}, device_id_type=MESH
        )
    pl.semaphore_wait(barrier, shards + groups - 2)


def remote(src, dst, send, recv, device):
    return pltpu.make_async_remote_copy(
        src_ref=src,
        dst_ref=dst,
        send_sem=send,
        recv_sem=recv,
        device_id=device,
        device_id_type=MESH,
    )


def far_first(shards):
    return sorted(range(1, shards), key=lambda k: -min(k, shards - k))


def layer_kernel(
    shards, heads, groups,
    q_ref, k_ref, v_ref, list_ref, glob_ref, w_ref, out_ref,
    q_here, named, glob_all, q_all, k_all, v_all, list_all, list_here, w_here, glob_here, o_here, att, acc,
    send_sem, recv_sem, pass_send, pass_recv, w_send, w_recv, own_sem,
    o_send, o_recv, side_send, side_recv, half_send, half_recv,
):
    me = lax.axis_index("seq")
    group = lax.axis_index("heads")
    rows, width = out_ref.shape
    depth = w_ref.shape[0]
    share = shards // heads
    piece = rows // share
    blocks = rows // BLOCK
    local = blocks // share
    last = shards * blocks - 1
    scale = DH ** (-0.5)
    nt = (((1,), (1,)), ((), ()))
    my_head = lax.div(me, share)
    my_part = lax.rem(me, share)
    pairs = ((k_ref, k_all), (v_ref, v_all))
    count = len(pairs)

    def window(src, head, part):
        return src.at[
            pl.ds(part * local, local), :, pl.ds(pl.multiple_of(head * DH, DH), DH)
        ]

    def landing(dst, source, part):
        return dst.at[pl.ds(source * blocks + part * local, local)]

    load_q = pltpu.make_async_copy(q_ref, q_here, own_sem.at[0])
    load_q.start()
    own_kv = [
        pltpu.make_async_copy(
            window(src, my_head, my_part), landing(dst, me, my_part), own_sem.at[1 + t]
        )
        for t, (src, dst) in enumerate(pairs)
    ]
    own_q = pltpu.make_async_copy(
        window(q_ref, my_head, my_part), q_all.at[me], own_sem.at[3]
    )
    own_list = pltpu.make_async_copy(list_ref.at[my_head], list_all.at[me], own_sem.at[4])
    own_w = pltpu.make_async_copy(
        w_ref.at[:, pl.ds(pl.multiple_of(group * width, width), width)],
        w_here.at[group],
        own_sem.at[5],
    )
    for copy in (*own_kv, own_q, own_list, own_w):
        copy.start()
    load_q.wait()
    for r in range(GLOBAL):
        picked = q_here[lax.rem(glob_ref[r], blocks)]
        for head in range(heads):
            named[head, r] = picked[:, head * DH : (head + 1) * DH]
    greet(shards, groups, me, group)

    def weight_rows(of, part):
        slab = depth // share
        return w_here.at[of, pl.ds(pl.multiple_of(part * slab, slab), slab), :]

    weights = {}
    for k in range(1, groups):
        to = lax.rem(group + k, groups)
        slab = depth // share
        weights[k] = remote(
            w_ref.at[
                pl.ds(pl.multiple_of(my_part * slab, slab), slab),
                pl.ds(pl.multiple_of(to * width, width), width),
            ],
            weight_rows(group, my_part),
            w_send.at[0, k],
            w_recv.at[0, k],
            {"heads": to},
        )
        weights[k].start()

    sends = {}
    for k in far_first(shards):
        to = lax.rem(me + k, shards)
        head, part = lax.div(to, share), lax.rem(to, share)
        for t, (src, dst) in enumerate(pairs):
            sends[k, t] = remote(
                window(src, head, part),
                landing(dst, me, part),
                send_sem.at[k, t],
                recv_sem.at[k, t],
                {"seq": to},
            )
            sends[k, t].start()
    for k in far_first(shards):
        to = lax.rem(me + k, shards)
        head, part = lax.div(to, share), lax.rem(to, share)
        sends[k, count] = remote(
            named.at[head, part],
            glob_all.at[me, part],
            send_sem.at[k, count],
            recv_sem.at[k, count],
            {"seq": to},
        )
        sends[k, count + 1] = remote(
            list_ref.at[head],
            list_all.at[me],
            send_sem.at[k, count + 1],
            recv_sem.at[k, count + 1],
            {"seq": to},
        )
        for t in (count, count + 1):
            sends[k, t].start()
    own_glob = pltpu.make_async_copy(
        named.at[my_head, my_part], glob_all.at[me, my_part], own_sem.at[0]
    )
    own_glob.start()
    stride = 3 if shards % 3 else 1
    for i in range(1, shards):
        k = (shards - i * stride % shards) % shards
        to = lax.rem(me + k, shards)
        sends[k, count + 2] = remote(
            window(q_ref, lax.div(to, share), lax.rem(to, share)),
            q_all.at[me],
            send_sem.at[k, count + 2],
            recv_sem.at[k, count + 2],
            {"seq": to},
        )
        sends[k, count + 2].start()

    passed = []

    def hand_on(region, t, k):
        for j in range(1, share):
            partner = my_head * share + lax.rem(my_part + j, share)
            passed.append(
                remote(
                    region, region, pass_send.at[j, k, t], pass_recv.at[j, k, t], {"seq": partner}
                )
            )
            passed[-1].start()

    for k in [0] + far_first(shards):
        source = lax.rem(me + shards - k, shards)
        for t, (_, dst) in enumerate(pairs):
            if k == 0:
                own_kv[t].wait()
            else:
                sends[k, t].wait_recv()
            hand_on(landing(dst, source, my_part), t, k)
    for k in [0] + far_first(shards):
        source = lax.rem(me + shards - k, shards)
        if k == 0:
            own_glob.wait()
            own_list.wait()
        else:
            sends[k, count].wait_recv()
            sends[k, count + 1].wait_recv()
        hand_on(glob_all.at[source, my_part], count, k)
    told = pltpu.make_async_copy(list_all, list_here, own_sem.at[4])
    told.start()
    for k in range(1, groups):
        weights[k].wait_recv()
        of = lax.rem(group + groups - k, groups)
        for j in range(1, share):
            partner = my_head * share + lax.rem(my_part + j, share)
            weights[k, j] = remote(
                weight_rows(of, my_part),
                weight_rows(of, my_part),
                w_send.at[j, k],
                w_recv.at[j, k],
                {"seq": partner},
            )
            weights[k, j].start()
    for copy in passed:
        copy.wait_recv()
    told.wait()
    own_q.wait()

    glob_q = jnp.concatenate(
        [glob_all[lax.div(glob_ref[r], blocks), r] for r in range(GLOBAL)], axis=0
    )

    def step(c, carry):
        peak, total, mixed = carry
        at = pl.ds(c * blocks, blocks)
        scores = lax.dot_general(
            glob_q, k_all[at].reshape(rows, DH), nt, preferred_element_type=jnp.float32
        ) * scale
        top = jnp.maximum(peak, jnp.max(scores, axis=-1, keepdims=True))
        fade = jnp.exp(peak - top)
        heavy = jnp.exp(scores - top)
        total = total * fade + jnp.sum(heavy, axis=-1, keepdims=True)
        mixed = mixed * fade + jnp.dot(
            heavy.astype(jnp.bfloat16),
            v_all[at].reshape(rows, DH),
            preferred_element_type=jnp.float32,
        )
        return top, total, mixed

    size = GLOBAL * BLOCK
    _, total_glob, mixed_glob = lax.fori_loop(
        0,
        shards,
        step,
        (
            jnp.full((size, 1), -jnp.inf, jnp.float32),
            jnp.zeros((size, 1), jnp.float32),
            jnp.zeros((size, DH), jnp.float32),
        ),
    )
    glob_here[...] = mixed_glob / total_glob

    lanes = (3 + RANDOM + GLOBAL) * BLOCK
    column = lax.broadcasted_iota(jnp.int32, (1, lanes), 1) // BLOCK

    def one(i, s, j):
        here = my_part * local + j
        b = s * blocks + here
        listed = [jnp.maximum(b - 1, 0), b, jnp.minimum(b + 1, last)]
        for r in range(RANDOM):
            at = here * RANDOM + r
            listed.append(list_here[s, lax.div(at, 128), lax.rem(at, 128)])
        for r in range(GLOBAL):
            listed.append(glob_ref[r])
        keys = jnp.concatenate([k_all[x] for x in listed], axis=0)
        values = jnp.concatenate([v_all[x] for x in listed], axis=0)
        scores = lax.dot_general(
            q_all[s, j], keys, nt, preferred_element_type=jnp.float32
        ) * scale
        hidden = ((column == 0) & (b == 0)) | ((column == 2) & (b == last))
        scores = jnp.where(hidden, -jnp.inf, scores)
        peak = jnp.max(scores, axis=-1, keepdims=True)
        heavy = jnp.exp(scores - peak)
        total = jnp.sum(heavy, axis=-1, keepdims=True)
        mixed = jnp.dot(heavy.astype(jnp.bfloat16), values, preferred_element_type=jnp.float32)
        result = mixed / total
        for r in range(GLOBAL):
            apart = jnp.full((BLOCK, DH), b, jnp.int32) - jnp.full((BLOCK, DH), glob_ref[r], jnp.int32)
            result = jnp.where(apart == 0, glob_here[r * BLOCK : (r + 1) * BLOCK, :], result)
        o_here[i, j * BLOCK : (j + 1) * BLOCK, :] = result.astype(jnp.bfloat16)

    across = lax.div(group, SIDE)
    along = lax.rem(group, SIDE)
    sides = (across * SIDE + (1 - along), (1 - across) * SIDE + along)
    diagonal = (1 - across) * SIDE + (1 - along)

    def spot(of, source):
        part = lax.rem(source, share)
        return att.at[
            of,
            pl.ds(pl.multiple_of(part * piece, piece), piece),
            pl.ds(pl.multiple_of(lax.div(source, share) * DH, DH), DH),
        ]

    def ahead(i):
        return lax.rem(me + lax.rem(i * stride, shards), shards)

    def behind(i):
        return lax.rem(me + shards - lax.rem(i * stride, shards), shards)

    def asked(i):
        k = lax.rem(shards - lax.rem(i * stride, shards), shards)
        return remote(
            window(q_ref, 0, 0),
            q_all.at[me],
            send_sem.at[k, count + 2],
            recv_sem.at[k, count + 2],
            {"seq": ahead(i)},
        )

    def kept():
        return pltpu.make_async_copy(o_here.at[0], spot(group, me), own_sem.at[0])

    def back(i):
        return remote(
            o_here.at[i], spot(group, me), o_send.at[i], o_recv.at[i], {"seq": ahead(i)}
        )

    def sideways(i, n):
        region = spot(group, behind(i))
        return remote(
            region, region, side_send.at[n, i], side_recv.at[n, i], {"heads": sides[n]}
        )

    def corner(i, n):
        half = piece // 2
        region = spot(sides[n], behind(i)).at[n * half : (n + 1) * half, :]
        return remote(
            region, region, half_send.at[n, i], half_recv.at[n, i], {"heads": sides[1 - n]}
        )

    @pl.loop(0, shards + LAG)
    def _(i):
        @pl.when(i < shards)
        def _():
            s = ahead(i)

            @pl.when(i > 0)
            def _():
                asked(i).wait_recv()

            for j in range(local):
                one(i, s, j)

            @pl.when(i == 0)
            def _():
                kept().start()

            @pl.when(i > 0)
            def _():
                back(i).start()

        @pl.when((i >= LAG) & (i < shards + LAG))
        def _():
            due = i - LAG

            @pl.when(due == 0)
            def _():
                kept().wait()

            @pl.when(due > 0)
            def _():
                back(due).wait_recv()

            for n in range(SIDE):
                sideways(due, n).start()

        @pl.when(i >= 2 * LAG)
        def _():
            due = i - 2 * LAG
            for n in range(SIDE):
                sideways(due, n).wait_recv()
                corner(due, n).start()

    own_w.wait()
    for k in range(1, groups):
        for j in range(1, share):
            weights[k, j].wait_recv()

    def project(parts, first, final):
        @pl.loop(0, share)
        def _(part):
            at = pl.ds(pl.multiple_of(part * piece, piece), piece)

            @pl.loop(0, width // TILE)
            def _(c):
                cols = pl.ds(pl.multiple_of(c * TILE, TILE), TILE)
                term = sum(
                    jnp.dot(
                        att[of, at, :], w_here[of, :, cols], preferred_element_type=jnp.float32
                    )
                    for of in parts
                )
                if not first:
                    term = term + acc[at, cols]
                if final:
                    out_ref[at, cols] = term.astype(out_ref.dtype)
                else:
                    acc[at, cols] = term

    project((group,), True, False)

    @pl.loop(shards - LAG, shards)
    def _(due):
        for n in range(SIDE):
            sideways(due, n).wait_recv()
            corner(due, n).start()

    project(sides, False, False)

    @pl.loop(0, shards)
    def _(i):
        for n in range(SIDE):
            corner(i, n).wait_recv()

    project((diagonal,), False, True)

    for copy in sends.values():
        copy.wait_send()
    for copy in passed:
        copy.wait_send()
    for copy in weights.values():
        copy.wait_send()

    @pl.loop(0, shards)
    def _(i):
        @pl.when(i > 0)
        def _():
            back(i).wait_send()

        for n in range(SIDE):
            sideways(i, n).wait_send()
            corner(i, n).wait_send()


def regrouped(queries, key_vectors, value_vectors, random_blocks, global_blocks, out_weight):
    shards = lax.axis_size("seq")
    groups = lax.axis_size("heads")
    rows, features = queries.shape
    heads = features // DH
    blocks = rows // BLOCK
    share = shards // heads
    piece = rows // share
    depth, model = out_weight.shape
    width = model // groups
    entries = blocks * RANDOM
    tall = -(-entries // 1024) * 8
    lists = jnp.pad(
        random_blocks.reshape(heads, entries), ((0, 0), (0, tall * 128 - entries))
    ).reshape(heads, tall, 128)
    dma = pltpu.SemaphoreType.DMA
    bf16 = jnp.bfloat16
    whole = pltpu.VMEM((shards * blocks, BLOCK, DH), bf16)
    split = (blocks, BLOCK, features)
    return pl.pallas_call(
        functools.partial(layer_kernel, shards, heads, groups),
        out_shape=jax.ShapeDtypeStruct((rows, width), bf16),
        in_specs=[ANY] * 4 + [pl.BlockSpec(memory_space=pltpu.SMEM), ANY],
        out_specs=pl.BlockSpec(memory_space=pltpu.VMEM),
        scratch_shapes=[
            pltpu.VMEM(split, bf16),
            pltpu.VMEM((heads, GLOBAL, BLOCK, DH), bf16),
            pltpu.VMEM((shards, GLOBAL, BLOCK, DH), bf16),
            pltpu.VMEM((shards, blocks // share, BLOCK, DH), bf16),
            whole,
            whole,
            pltpu.VMEM((shards, tall, 128), jnp.int32),
            pltpu.SMEM((shards, tall, 128), jnp.int32),
            pltpu.VMEM((groups, depth, width), bf16),
            pltpu.VMEM((GLOBAL * BLOCK, DH), jnp.float32),
            pltpu.VMEM((shards, piece, DH), bf16),
            pltpu.VMEM((groups, rows, features), bf16),
            pltpu.VMEM((rows, width), jnp.float32),
            dma((shards, 5)),
            dma((shards, 5)),
            dma((share, shards, 3)),
            dma((share, shards, 3)),
            dma((share, groups)),
            dma((share, groups)),
            dma((6,)),
            dma((shards,)),
            dma((shards,)),
            dma((SIDE, shards)),
            dma((SIDE, shards)),
            dma((SIDE, shards)),
            dma((SIDE, shards)),
        ],
        compiler_params=pltpu.CompilerParams(
            collective_id=0, has_side_effects=True, vmem_limit_bytes=VMEM_BYTES
        ),
        name="layer",
    )(
        queries.reshape(split),
        key_vectors.reshape(split),
        value_vectors.reshape(split),
        lists,
        global_blocks,
        out_weight,
    )


def on_device(queries, key_vectors, value_vectors, random_blocks, global_blocks, out_weight):
    shards = lax.axis_size("seq")
    groups = lax.axis_size("heads")
    rows, features = queries.shape
    heads = features // DH
    whole_heads = shards % heads == 0 and (rows // BLOCK) % (shards // heads) == 0
    body = regrouped if whole_heads and groups == SIDE * SIDE and shards == heads * GLOBAL else requested
    return body(queries, key_vectors, value_vectors, random_blocks, global_blocks, out_weight)


def solution(mesh):
    placed = (
        P("seq", "heads"),
        P("seq", "heads"),
        P("seq", "heads"),
        P("heads", "seq", None),
        P(),
        P("heads", None),
    )
    return jax.shard_map(
        on_device, mesh=mesh, in_specs=placed, out_specs=P("seq", "heads"), check_vma=False
    )
```
